256 devices in a mesh: tm: 64 (over y, z, core), tile: 4 (over x).
Axes of the slice: x: 4, y: 4, z: 8, core: 2. Of those that a mesh axis runs over, the one named last changes fastest.
Arguments:
- increment: float32 [64, 137, 8, 1024], P('tm', None, None, 'tile'), may hold values from -6 to 6
- vertical: float32 [64, 137, 137], P('tm'), may hold values from -0.5 to 0.5
- east_wind: float32 [64, 8, 1024], P('tm', None, 'tile'), may hold values from -0.5 to 0.5
- north_wind: float32 [64, 8, 1024], P('tm', None, 'tile'), may hold values from -0.5 to 0.5
- error_weight: float32 [64, 137], P('tm'), may hold values from 0.5 to 4
- decay: float32 [64, 137], P('tm'), may hold values from 0 to 1
- forcing: float32 [64, 137], P('tm'), may hold values from -3 to 3
- obs_column: int32 [64, 4096], P('tm', 'tile'), may hold values from 0 to 2047
- obs_count: int32 [64, 256], P('tm', 'tile'), may hold values from 0 to 16, as said below
- obs_weight: float32 [64, 137, 4096], P('tm', None, 'tile'), may hold values from -0.5 to 0.5
- obs_rinv: float32 [64, 4096], P('tm', 'tile'), may hold values from 0.3 to 3
- obs_depart: float32 [64, 4096], P('tm', 'tile'), may hold values from -6 to 6
Outputs:
- grad_increment: float32 [64, 137, 8, 1024], P('tm', None, None, 'tile')
- grad_forcing: float32 [64, 137], P('tm')
- obs_equiv: float32 [64, 4096], P('tm', 'tile')
The draws below stay inside these ranges and needn't reach their ends.
Inputs may be any that keep to these rules, and one draw needn't show every extreme that they name: `obs_count`: every sub-window tile sends 16 live slots to some owner, and in each tile one owner receives 16 from every sub-window. `obs_column`: A column is latitude row times 256 plus the longitude within the tile; slots at or past the count are unused.
All inputs are finite; a program needn't handle non-finite values.
Results may differ from the reference program's by a relative error of at most 0.0003.
Values sent between devices are 32-bit elements; how exact they have to be, the bound alone decides.
A program may use at most 64 MiB of HBM per device.

```python
import math
import jax
import jax.numpy as jnp
from jax import lax

LEV = 137
LAT = 8
TILE_LONGITUDES = 256
CAP = 16
STEPS = 2
SUB_WINDOWS = 64
LON = 1024
N_TM = 64
N_TILE = 4


def draw_decay(key, part):
    random_keys = jax.random.split(jax.random.fold_in(key, 11), 6)
    share = 0.5
    slower = jax.random.uniform(random_keys[0], (LEV,)) < share
    keeping = jax.random.uniform(random_keys[1], (LEV,), minval=0.1, maxval=0.5)
    gentle_decay_rate = jnp.exp(jnp.log(keeping) / SUB_WINDOWS)
    fast_rate = jax.random.uniform(random_keys[2], (LEV,), minval=0.2, maxval=0.6)
    base_rate = jnp.where(slower, gentle_decay_rate, fast_rate)
    powers = jnp.exp(jax.random.uniform(random_keys[3], (SUB_WINDOWS, LEV), minval=jnp.log(0.5), maxval=jnp.log(2.0)))
    forcing_pulses = jax.random.uniform(random_keys[4], (SUB_WINDOWS, 1)) < 3.0 / SUB_WINDOWS
    scale_multiplier = jnp.where(forcing_pulses, jax.random.uniform(random_keys[5], (SUB_WINDOWS, 1), minval=0.5, maxval=0.8), 1.0)
    return (base_rate[None, :] ** powers * scale_multiplier).astype(jnp.float32)


def draw_obs_count(key, part):
    random_keys = jax.random.split(jax.random.fold_in(key, 23), 2)
    counts = jax.random.randint(random_keys[0], (SUB_WINDOWS, N_TILE, N_TM), 0, CAP + 1)
    busiest = jax.random.randint(random_keys[1], (N_TILE,), 0, N_TM)
    marked = jnp.arange(N_TM)[None, None, :] == busiest[None, :, None]
    return jnp.where(marked, CAP, counts).reshape(SUB_WINDOWS, N_TILE * N_TM).astype(jnp.int32)


def plant(array, stream_key, low, top_value):
    longest = array.shape.index(max(array.shape))
    spots = []
    for shift in (0, 1):
        where = [jax.random.randint(jax.random.fold_in(stream_key, axis), (), 0, length) for axis, length in enumerate(array.shape)]
        where[longest] = (where[longest] + shift) % array.shape[longest]
        spots.append(tuple(where))
    return array.at[spots[0]].set(low).at[spots[1]].set(top_value)


def block_levels(key, extent, pieces, least, largest):
    def one(axis_at, blocks):
        steps = jax.random.uniform(jax.random.fold_in(jax.random.fold_in(key, 6), axis_at), (blocks,), jnp.float32, least / len(pieces), largest / len(pieces))
        return jnp.repeat(jnp.exp(steps), extent[axis_at] // blocks).reshape((-1,) + (1,) * (len(extent) - axis_at - 1))

    gain = one(*pieces[0])
    for cut in pieces[1:]:
        gain = gain * one(*cut)
    return gain


def noise(own_key, dims, spread, bound, shards=(), kind=jnp.bfloat16):
    loudness = block_levels(own_key, dims, shards, -0.22, 0.18) if shards else 1.0
    array = jax.random.normal(own_key, dims, jnp.float32) * spread * loudness
    return jnp.minimum(jnp.maximum(array, -bound), bound).astype(kind)


def setup_inputs(seed: int = 0) -> dict:
    streams_of = jax.random.split(jax.random.key(seed), 13)
    increment = noise(streams_of[0], (SUB_WINDOWS, LEV, LAT, LON), 1.0, 6.0, ((0, 64), (3, 4)), jnp.float32)
    vertical = noise(streams_of[1], (SUB_WINDOWS, LEV, LEV), LEV ** -0.5, 0.5, ((0, 64),), jnp.float32)
    east_wind = jnp.clip(jax.random.uniform(streams_of[2], (SUB_WINDOWS, LAT, LON), jnp.float32, -0.5, 0.5) * block_levels(streams_of[2], (SUB_WINDOWS, LAT, LON), ((0, 64), (2, 4)), -0.4, 0.0), -0.5, 0.5)
    north_wind = jnp.clip(jax.random.uniform(streams_of[3], (SUB_WINDOWS, LAT, LON), jnp.float32, -0.5, 0.5) * block_levels(streams_of[3], (SUB_WINDOWS, LAT, LON), ((0, 64), (2, 4)), -0.4, 0.0), -0.5, 0.5)
    error_weight = jnp.clip(jnp.exp(math.log(4.0) - 2.0794415 * jax.random.uniform(streams_of[4], (SUB_WINDOWS, LEV), jnp.float32) ** block_levels(streams_of[4], (SUB_WINDOWS, LEV), ((0, 64),), -0.2, 0.2)), 0.5, 4.0)
    decay = draw_decay(jax.random.fold_in(streams_of[12], 71), 0)
    forcing = noise(streams_of[6], (SUB_WINDOWS, LEV), 0.5, 3.0, ((0, 64),), jnp.float32)
    obs_column = plant(jax.random.randint(streams_of[7], (SUB_WINDOWS, N_TILE * N_TM * CAP), 0, LAT * TILE_LONGITUDES), jax.random.fold_in(streams_of[7], 1), 0, (LAT * TILE_LONGITUDES) - 1).astype(jnp.int32)
    obs_count = draw_obs_count(jax.random.fold_in(streams_of[12], 71), 0)
    obs_weight = noise(streams_of[9], (SUB_WINDOWS, LEV, N_TILE * N_TM * CAP), LEV ** -0.5, 0.5, ((0, 64), (2, 4)), jnp.float32)
    obs_rinv = jnp.clip(jnp.exp(math.log(3.0) - 2.3025851 * jax.random.uniform(streams_of[10], (SUB_WINDOWS, N_TILE * N_TM * CAP), jnp.float32) ** block_levels(streams_of[10], (SUB_WINDOWS, N_TILE * N_TM * CAP), ((0, 64), (1, 4)), -0.2, 0.2)), 0.3, 3.0)
    obs_depart = noise(streams_of[11], (SUB_WINDOWS, N_TILE * N_TM * CAP), 1.0, 6.0, ((0, 64), (1, 4)), jnp.float32)
    return {"increment": increment, "vertical": vertical, "east_wind": east_wind, "north_wind": north_wind, "error_weight": error_weight, "decay": decay, "forcing": forcing, "obs_column": obs_column, "obs_count": obs_count, "obs_weight": obs_weight, "obs_rinv": obs_rinv, "obs_depart": obs_depart}


def advance(field, vertical, eastward, northward):
    west_side = jnp.roll(field, 1, axis=2)
    east_side = jnp.roll(field, -1, axis=2)
    padded = jnp.pad(field, ((0, 0), (1, 1), (0, 0)))
    mixing = jnp.dot(vertical, field.reshape(field.shape[0], -1), precision=lax.Precision.HIGHEST, preferred_element_type=jnp.float32).reshape(field.shape)
    return field + mixing + eastward[None] * (west_side - east_side) * 0.5 + northward[None] * (padded[:, :-2] - padded[:, 2:]) * 0.5


def retreat(costate, vertical, eastward, northward):
    zonal = eastward[None] * costate
    lon_part = (jnp.roll(zonal, -1, axis=2) - jnp.roll(zonal, 1, axis=2)) * 0.5
    merid = jnp.pad(northward[None] * costate, ((0, 0), (1, 1), (0, 0)))
    lat_part = (merid[:, 2:] - merid[:, :-2]) * 0.5
    mixing = jnp.dot(vertical.T, costate.reshape(costate.shape[0], -1), precision=lax.Precision.HIGHEST, preferred_element_type=jnp.float32).reshape(costate.shape)
    return costate + mixing + lon_part + lat_part


def run_forward(packed):
    field, vertical, eastward, northward = packed
    for section in range(STEPS):
        field = advance(field, vertical, eastward, northward)
    return field


def run_backward(packed):
    field, vertical, eastward, northward = packed
    for section in range(STEPS):
        field = retreat(field, vertical, eastward, northward)
    return field


def take_columns(field, columns):
    return jnp.take(field, columns, axis=1)


def add_columns(values, columns):
    return jnp.zeros((LEV, LAT * TILE_LONGITUDES), jnp.float32).at[:, columns].add(values)


def reference(increment, vertical, east_wind, north_wind, error_weight, decay, forcing, obs_column, obs_count, obs_weight, obs_rinv, obs_depart):
    def forward_step(carry, pair):
        rate, push = pair
        nexts = rate * carry + push
        return nexts, nexts

    _, bias = lax.scan(forward_step, jnp.zeros((LEV,), jnp.float32), (decay, forcing))
    start = increment + bias[:, :, None, None]
    final = lax.map(run_forward, (start, vertical, east_wind, north_wind))
    earlier = jnp.concatenate([jnp.zeros_like(final[:1]), final[:-1]], axis=0)
    weighted = error_weight[:, :, None, None] * (start - earlier)

    slots = N_TM * CAP
    tiled = final.reshape(SUB_WINDOWS, LEV, LAT, N_TILE, TILE_LONGITUDES).transpose(0, 3, 1, 2, 4).reshape(SUB_WINDOWS, N_TILE, LEV, LAT * TILE_LONGITUDES)
    columns = obs_column.reshape(SUB_WINDOWS, N_TILE, slots)
    counts = obs_count.reshape(SUB_WINDOWS, N_TILE, N_TM)
    live = (jnp.arange(CAP)[None, None, None, :] < counts[..., None]).astype(jnp.float32).reshape(SUB_WINDOWS, N_TILE, slots)
    profiles = jax.vmap(jax.vmap(take_columns))(tiled, columns) * live[:, :, None, :]
    owned = profiles.reshape(SUB_WINDOWS, N_TILE, LEV, SUB_WINDOWS, CAP).transpose(3, 1, 2, 0, 4)
    weight_values = obs_weight.reshape(SUB_WINDOWS, LEV, N_TILE, SUB_WINDOWS, CAP).transpose(0, 2, 1, 3, 4)
    equiv = jnp.sum(weight_values * owned, axis=2)
    misfit = obs_rinv.reshape(SUB_WINDOWS, N_TILE, SUB_WINDOWS, CAP) * (equiv - obs_depart.reshape(SUB_WINDOWS, N_TILE, SUB_WINDOWS, CAP))
    adjoint_prof = (weight_values * misfit[:, :, None]).transpose(3, 1, 2, 0, 4).reshape(SUB_WINDOWS, N_TILE, LEV, slots) * live[:, :, None, :]
    adjoint_tiles = jax.vmap(jax.vmap(add_columns))(adjoint_prof, columns)
    adjoint_end = adjoint_tiles.reshape(SUB_WINDOWS, N_TILE, LEV, LAT, TILE_LONGITUDES).transpose(0, 2, 3, 1, 4).reshape(SUB_WINDOWS, LEV, LAT, LON)

    later = jnp.concatenate([weighted[1:], jnp.zeros_like(weighted[:1])], axis=0)
    costate = adjoint_end - later
    back = lax.map(run_backward, (costate, vertical, east_wind, north_wind))
    grad_increment = weighted + back
    column_mean = jnp.mean(grad_increment, axis=(2, 3))

    def backward_step(carry, pair):
        rate, mean_grad = pair
        total = mean_grad + carry
        return rate * total, total

    _, grad_forcing = lax.scan(backward_step, jnp.zeros((LEV,), jnp.float32), (decay, column_mean), reverse=True)
    return grad_increment, grad_forcing, equiv.reshape(SUB_WINDOWS, N_TILE * SUB_WINDOWS * CAP)
```

```python
import jax
import jax.numpy as jnp
from jax import lax
from jax.sharding import PartitionSpec as P

STEPS = 2


def padded_2(block, sides, width):
    for axis, dim in sides:
        count = lax.axis_size(axis)
        forward = [(i, i + 1) for i in range(count - 1)]
        forward.append((count - 1, 0))
        backward = [(target, source) for source, target in forward]
        low = lax.ppermute(
            lax.slice_in_dim(block, block.shape[dim] - width, None, axis=dim), axis, forward
        )
        high = lax.ppermute(lax.slice_in_dim(block, 0, width, axis=dim), axis, backward)
        block = jnp.concatenate([low, block, high], axis=dim)
    return block


def gathered(value, axis):
    count = lax.axis_size(axis)
    spread = jnp.broadcast_to(value[None], (count,) + value.shape)
    return lax.all_to_all(spread, axis, 0, 0, tiled=True)


def passed_along(value, axis, by):
    peers = lax.axis_size(axis)
    pairs = [(i, i + by) for i in range(peers) if 0 <= i + by < peers]
    return lax.ppermute(value, axis, pairs)


def with_rim(field):
    return padded_2(field, (("tile", 2),), 1)


def advance(field, vertical, eastward, northward):
    widened = with_rim(field)
    padded = jnp.pad(field, ((0, 0), (1, 1), (0, 0)))
    mixing = jnp.dot(
        vertical,
        field.reshape(field.shape[0], -1),
        precision=lax.Precision.HIGHEST,
        preferred_element_type=jnp.float32,
    ).reshape(field.shape)
    return (
        field
        + mixing
        + eastward[None] * (widened[:, :, :-2] - widened[:, :, 2:]) * 0.5
        + northward[None] * (padded[:, :-2] - padded[:, 2:]) * 0.5
    )


def retreat(costate, vertical, eastward, northward):
    zonal = with_rim(eastward[None] * costate)
    lon_part = (zonal[:, :, 2:] - zonal[:, :, :-2]) * 0.5
    merid = jnp.pad(northward[None] * costate, ((0, 0), (1, 1), (0, 0)))
    lat_part = (merid[:, 2:] - merid[:, :-2]) * 0.5
    mixing = jnp.dot(
        vertical.T,
        costate.reshape(costate.shape[0], -1),
        precision=lax.Precision.HIGHEST,
        preferred_element_type=jnp.float32,
    ).reshape(costate.shape)
    return costate + mixing + lon_part + lat_part


def bias_of(rates, pushes, mine):
    order = lax.broadcasted_iota(jnp.int32, rates.shape, 0)
    masked = jnp.where(order <= mine, rates, 1.0)
    through = lax.cumprod(masked, axis=0, reverse=True)
    after = jnp.concatenate([through[1:], jnp.ones_like(through[:1])], axis=0)
    return jnp.sum(jnp.where(order <= mine, after * pushes, 0.0), axis=0)


def carried_back(rates, means, mine):
    order = lax.broadcasted_iota(jnp.int32, rates.shape, 0)
    masked = jnp.where(order > mine, rates, 1.0)
    through = lax.cumprod(masked, axis=0)
    return jnp.sum(jnp.where(order >= mine, through * means, 0.0), axis=0)


def shards(
    increment,
    vertical,
    east_wind,
    north_wind,
    error_weight,
    decay,
    forcing,
    obs_column,
    obs_count,
    obs_weight,
    obs_rinv,
    obs_depart,
):
    levels = increment.shape[1]
    lat_rows = increment.shape[2]
    lon_cols = increment.shape[3]
    tm_count = lax.axis_size("tm")
    slot_total = obs_column.shape[1]
    slot_cap = slot_total // tm_count
    mine = lax.axis_index("tm")
    both = gathered(jnp.stack([decay[0], forcing[0]]), "tm")
    all_rates = both[:, 0]
    bias = bias_of(all_rates, both[:, 1], mine)
    start = increment[0] + bias[:, None, None]
    mixer = vertical[0]
    eastward = east_wind[0]
    northward = north_wind[0]
    final = start
    for section in range(STEPS):
        final = advance(final, mixer, eastward, northward)
    earlier = passed_along(final, "tm", 1)
    weighted = error_weight[0][:, None, None] * (start - earlier)
    flattened = final.reshape(levels, lat_rows * lon_cols)
    columns = obs_column[0]
    live = (jnp.arange(slot_total) % slot_cap < jnp.repeat(obs_count[0], slot_cap)).astype(
        jnp.float32
    )
    profiles = jnp.take(flattened, columns, axis=1) * live[None, :]
    arrived = lax.all_to_all(profiles, "tm", split_axis=1, concat_axis=1, tiled=True)
    equiv = jnp.sum(obs_weight[0] * arrived, axis=0)
    misfit = obs_rinv[0] * (equiv - obs_depart[0])
    returned = lax.all_to_all(
        obs_weight[0] * misfit[None, :], "tm", split_axis=1, concat_axis=1, tiled=True
    )
    adjoint_prof = returned * live[None, :]
    adjoint_end = (
        jnp.zeros((levels, lat_rows * lon_cols), jnp.float32)
        .at[:, columns]
        .add(adjoint_prof)
        .reshape(levels, lat_rows, lon_cols)
    )
    following = passed_along(weighted, "tm", -1)
    costate = adjoint_end - following
    for section in range(STEPS):
        costate = retreat(costate, mixer, eastward, northward)
    gradient = weighted + costate
    partial_mean = jnp.sum(gradient, axis=(1, 2)) / (lat_rows * lon_cols * lax.axis_size("tile"))
    column_mean = lax.psum(partial_mean, "tile")
    grad_forcing = carried_back(all_rates, gathered(column_mean, "tm"), mine)
    return (gradient[None], grad_forcing[None], equiv[None])


def solution(mesh):
    placed = (
        P("tm", None, None, "tile"),
        P("tm", None, None),
        P("tm", None, "tile"),
        P("tm", None, "tile"),
        P("tm", None),
        P("tm", None),
        P("tm", None),
        P("tm", "tile"),
        P("tm", "tile"),
        P("tm", None, "tile"),
        P("tm", "tile"),
        P("tm", "tile"),
    )
    return jax.shard_map(
        shards,
        mesh=mesh,
        in_specs=placed,
        out_specs=(P("tm", None, None, "tile"), P("tm", None), P("tm", "tile")),
        check_vma=False,
    )
```

```python
import jax
import jax.numpy as jnp
from jax import lax
from jax.sharding import PartitionSpec as P

STEPS = 2


def padded_2(block, sides, width):
    for axis, dim in sides:
        count = lax.axis_size(axis)
        forward = [(i, i + 1) for i in range(count - 1)]
        forward.append((count - 1, 0))
        backward = [(target, source) for source, target in forward]
        low = lax.ppermute(
            lax.slice_in_dim(block, block.shape[dim] - width, None, axis=dim), axis, forward
        )
        high = lax.ppermute(lax.slice_in_dim(block, 0, width, axis=dim), axis, backward)
        block = jnp.concatenate([low, block, high], axis=dim)
    return block


def gathered(value, axis):
    count = lax.axis_size(axis)
    spread = jnp.broadcast_to(value[None], (count,) + value.shape)
    return lax.all_to_all(spread, axis, 0, 0, tiled=True)


def passed_along(value, axis, by):
    peers = lax.axis_size(axis)
    pairs = [(i, i + by) for i in range(peers) if 0 <= i + by < peers]
    return lax.ppermute(value, axis, pairs)


def with_rim(field):
    return padded_2(field, (("tile", 2),), 1)


def advance(field, vertical, eastward, northward):
    widened = with_rim(field)
    padded = jnp.pad(field, ((0, 0), (1, 1), (0, 0)))
    mixing = jnp.dot(
        vertical,
        field.reshape(field.shape[0], -1),
        precision=lax.Precision.HIGHEST,
        preferred_element_type=jnp.float32,
    ).reshape(field.shape)
    return (
        field
        + mixing
        + eastward[None] * (widened[:, :, :-2] - widened[:, :, 2:]) * 0.5
        + northward[None] * (padded[:, :-2] - padded[:, 2:]) * 0.5
    )


def retreat(costate, vertical, eastward, northward):
    zonal = with_rim(eastward[None] * costate)
    lon_part = (zonal[:, :, 2:] - zonal[:, :, :-2]) * 0.5
    merid = jnp.pad(northward[None] * costate, ((0, 0), (1, 1), (0, 0)))
    lat_part = (merid[:, 2:] - merid[:, :-2]) * 0.5
    mixing = jnp.dot(
        vertical.T,
        costate.reshape(costate.shape[0], -1),
        precision=lax.Precision.HIGHEST,
        preferred_element_type=jnp.float32,
    ).reshape(costate.shape)
    return costate + mixing + lon_part + lat_part


def bias_of(rates, pushes, mine):
    order = lax.broadcasted_iota(jnp.int32, rates.shape, 0)
    masked = jnp.where(order <= mine, rates, 1.0)
    through = lax.cumprod(masked, axis=0, reverse=True)
    after = jnp.concatenate([through[1:], jnp.ones_like(through[:1])], axis=0)
    return jnp.sum(jnp.where(order <= mine, after * pushes, 0.0), axis=0)


def carried_back(rates, means, mine):
    order = lax.broadcasted_iota(jnp.int32, rates.shape, 0)
    masked = jnp.where(order > mine, rates, 1.0)
    through = lax.cumprod(masked, axis=0)
    return jnp.sum(jnp.where(order >= mine, through * means, 0.0), axis=0)


def shards(
    increment,
    vertical,
    east_wind,
    north_wind,
    error_weight,
    decay,
    forcing,
    obs_column,
    obs_count,
    obs_weight,
    obs_rinv,
    obs_depart,
):
    levels = increment.shape[1]
    lat_rows = increment.shape[2]
    lon_cols = increment.shape[3]
    tm_count = lax.axis_size("tm")
    slot_total = obs_column.shape[1]
    slot_cap = slot_total // tm_count
    mine = lax.axis_index("tm")
    both = gathered(jnp.stack([decay[0], forcing[0]]), "tm")
    all_rates = both[:, 0]
    bias = bias_of(all_rates, both[:, 1], mine)
    start = increment[0] + bias[:, None, None]
    mixer = vertical[0]
    eastward = east_wind[0]
    northward = north_wind[0]
    final = start
    for section in range(STEPS):
        final = advance(final, mixer, eastward, northward)
    earlier = passed_along(final, "tm", 1)
    weighted = error_weight[0][:, None, None] * (start - earlier)
    flattened = final.reshape(levels, lat_rows * lon_cols)
    columns = obs_column[0]
    live = (jnp.arange(slot_total) % slot_cap < jnp.repeat(obs_count[0], slot_cap)).astype(
        jnp.float32
    )
    weights = lax.all_to_all(obs_weight[0], "tm", split_axis=1, concat_axis=1, tiled=True)
    profiles = jnp.take(flattened, columns, axis=1) * live[None, :]
    seen = jnp.sum(weights * profiles, axis=0)
    equiv = lax.all_to_all(seen, "tm", split_axis=0, concat_axis=0, tiled=True)
    misfit = obs_rinv[0] * (equiv - obs_depart[0])
    returned = weights * lax.all_to_all(misfit, "tm", split_axis=0, concat_axis=0, tiled=True)
    adjoint_prof = returned * live[None, :]
    adjoint_end = (
        jnp.zeros((levels, lat_rows * lon_cols), jnp.float32)
        .at[:, columns]
        .add(adjoint_prof)
        .reshape(levels, lat_rows, lon_cols)
    )
    following = passed_along(weighted, "tm", -1)
    costate = adjoint_end - following
    for section in range(STEPS):
        costate = retreat(costate, mixer, eastward, northward)
    gradient = weighted + costate
    partial_mean = jnp.sum(gradient, axis=(1, 2)) / (lat_rows * lon_cols * lax.axis_size("tile"))
    column_mean = lax.psum(partial_mean, "tile")
    grad_forcing = carried_back(all_rates, gathered(column_mean, "tm"), mine)
    return (gradient[None], grad_forcing[None], equiv[None])


def solution(mesh):
    placed = (
        P("tm", None, None, "tile"),
        P("tm", None, None),
        P("tm", None, "tile"),
        P("tm", None, "tile"),
        P("tm", None),
        P("tm", None),
        P("tm", None),
        P("tm", "tile"),
        P("tm", "tile"),
        P("tm", None, "tile"),
        P("tm", "tile"),
        P("tm", "tile"),
    )
    return jax.shard_map(
        shards,
        mesh=mesh,
        in_specs=placed,
        out_specs=(P("tm", None, None, "tile"), P("tm", None), P("tm", "tile")),
        check_vma=False,
    )
```

```python
import jax
import jax.numpy as jnp
from jax import lax
from jax.sharding import PartitionSpec as P


STEPS = 2


def padded_2(block, sides, width):
    for axis, dim in sides:
        count = lax.axis_size(axis)
        forward = [(i, i + 1) for i in range(count - 1)]
        forward.append((count - 1, 0))
        backward = [(target, source) for source, target in forward]
        low = lax.ppermute(
            lax.slice_in_dim(block, block.shape[dim] - width, None, axis=dim), axis, forward
        )
        high = lax.ppermute(lax.slice_in_dim(block, 0, width, axis=dim), axis, backward)
        block = jnp.concatenate([low, block, high], axis=dim)
    return block


def gathered(value, axis):
    count = lax.axis_size(axis)
    spread = jnp.broadcast_to(value[None], (count,) + value.shape)
    return lax.all_to_all(spread, axis, 0, 0, tiled=True)


def passed_along(value, axis, by):
    peers = lax.axis_size(axis)
    pairs = [(i, i + by) for i in range(peers) if 0 <= i + by < peers]
    return lax.ppermute(value, axis, pairs)


def with_rim(field):
    return padded_2(field, (("tile", 2),), 1)


def advance(field, vertical, eastward, northward):
    widened = with_rim(field)
    padded = jnp.pad(field, ((0, 0), (1, 1), (0, 0)))
    mixing = jnp.dot(
        vertical,
        field.reshape(field.shape[0], -1),
        precision=lax.Precision.HIGHEST,
        preferred_element_type=jnp.float32,
    ).reshape(field.shape)
    return (
        field
        + mixing
        + eastward[None] * (widened[:, :, :-2] - widened[:, :, 2:]) * 0.5
        + northward[None] * (padded[:, :-2] - padded[:, 2:]) * 0.5
    )


def retreat(costate, vertical, eastward, northward):
    zonal = with_rim(eastward[None] * costate)
    lon_part = (zonal[:, :, 2:] - zonal[:, :, :-2]) * 0.5
    merid = jnp.pad(northward[None] * costate, ((0, 0), (1, 1), (0, 0)))
    lat_part = (merid[:, 2:] - merid[:, :-2]) * 0.5
    mixing = jnp.dot(
        vertical.T,
        costate.reshape(costate.shape[0], -1),
        precision=lax.Precision.HIGHEST,
        preferred_element_type=jnp.float32,
    ).reshape(costate.shape)
    return costate + mixing + lon_part + lat_part


def bias_of(rates, pushes, mine):
    order = lax.broadcasted_iota(jnp.int32, rates.shape, 0)
    masked = jnp.where(order <= mine, rates, 1.0)
    through = lax.cumprod(masked, axis=0, reverse=True)
    after = jnp.concatenate([through[1:], jnp.ones_like(through[:1])], axis=0)
    return jnp.sum(jnp.where(order <= mine, after * pushes, 0.0), axis=0)


def carried_back(rates, means, mine):
    order = lax.broadcasted_iota(jnp.int32, rates.shape, 0)
    masked = jnp.where(order > mine, rates, 1.0)
    through = lax.cumprod(masked, axis=0)
    return jnp.sum(jnp.where(order >= mine, through * means, 0.0), axis=0)


def shards_body(
    increment,
    vertical,
    east_wind,
    north_wind,
    error_weight,
    decay,
    forcing,
    obs_column,
    obs_count,
    obs_weight,
    obs_rinv,
    obs_depart,
):
    levels = increment.shape[1]
    lat_rows = increment.shape[2]
    lon_cols = increment.shape[3]
    tm_count = lax.axis_size("tm")
    slot_total = obs_column.shape[1]
    slot_cap = slot_total // tm_count
    mine = lax.axis_index("tm")
    both = gathered(jnp.stack([decay[0], forcing[0]]), "tm")
    all_rates = both[:, 0]
    bias = bias_of(all_rates, both[:, 1], mine)
    start = increment[0] + bias[:, None, None]
    mixer = vertical[0]
    eastward = east_wind[0]
    northward = north_wind[0]
    weights = lax.all_to_all(obs_weight[0], "tm", split_axis=1, concat_axis=1, tiled=True)
    final = start
    for _ in range(STEPS):
        final = advance(final, mixer, eastward, northward)
    earlier = passed_along(final, "tm", 1)
    weighted = error_weight[0][:, None, None] * (start - earlier)
    flattened = final.reshape(levels, lat_rows * lon_cols)
    columns = obs_column[0]
    live = (jnp.arange(slot_total) % slot_cap < jnp.repeat(obs_count[0], slot_cap)).astype(
        jnp.float32
    )
    profiles = jnp.take(flattened, columns, axis=1) * live[None, :]
    seen = jnp.sum(weights * profiles, axis=0)
    equiv = lax.all_to_all(seen, "tm", split_axis=0, concat_axis=0, tiled=True)
    misfit = obs_rinv[0] * (equiv - obs_depart[0])
    returned = weights * lax.all_to_all(misfit, "tm", split_axis=0, concat_axis=0, tiled=True)
    adjoint_prof = returned * live[None, :]
    adjoint_end = (
        jnp.zeros((levels, lat_rows * lon_cols), jnp.float32)
        .at[:, columns]
        .add(adjoint_prof)
        .reshape(levels, lat_rows, lon_cols)
    )
    following = passed_along(weighted, "tm", -1)
    costate = adjoint_end - following
    for _ in range(STEPS):
        costate = retreat(costate, mixer, eastward, northward)
    gradient = weighted + costate
    partial_mean = jnp.sum(gradient, axis=(1, 2)) / (lat_rows * lon_cols * lax.axis_size("tile"))
    column_mean = lax.psum(partial_mean, "tile")
    grad_forcing = carried_back(all_rates, gathered(column_mean, "tm"), mine)
    return (gradient[None], grad_forcing[None], equiv[None])


def solution(mesh):
    placed = (
        P("tm", None, None, "tile"),
        P("tm", None, None),
        P("tm", None, "tile"),
        P("tm", None, "tile"),
        P("tm", None),
        P("tm", None),
        P("tm", None),
        P("tm", "tile"),
        P("tm", "tile"),
        P("tm", None, "tile"),
        P("tm", "tile"),
        P("tm", "tile"),
    )
    return jax.shard_map(
        shards_body,
        mesh=mesh,
        in_specs=placed,
        out_specs=(P("tm", None, None, "tile"), P("tm", None), P("tm", "tile")),
        check_vma=False,
    )
```

```python
import jax
import jax.numpy as jnp
from jax import lax
from jax.sharding import PartitionSpec as P


STEPS = 2


def padded_2(block, sides, width):
    for axis, dim in sides:
        count = lax.axis_size(axis)
        forward = [(i, i + 1) for i in range(count - 1)]
        forward.append((count - 1, 0))
        backward = [(target, source) for source, target in forward]
        low = lax.ppermute(
            lax.slice_in_dim(block, block.shape[dim] - width, None, axis=dim), axis, forward
        )
        high = lax.ppermute(lax.slice_in_dim(block, 0, width, axis=dim), axis, backward)
        block = jnp.concatenate([low, block, high], axis=dim)
    return block


def gathered(value, axis):
    count = lax.axis_size(axis)
    spread = jnp.broadcast_to(value[None], (count,) + value.shape)
    return lax.all_to_all(spread, axis, 0, 0, tiled=True)


def passed_along(value, axis, by):
    peers = lax.axis_size(axis)
    pairs = [(i, i + by) for i in range(peers) if 0 <= i + by < peers]
    return lax.ppermute(value, axis, pairs)


def with_rim(field):
    return padded_2(field, (("tile", 2),), 1)


def advance(field, vertical, eastward, northward):
    widened = with_rim(field)
    padded = jnp.pad(field, ((0, 0), (1, 1), (0, 0)))
    mixing = jnp.dot(
        vertical,
        field.reshape(field.shape[0], -1),
        precision=lax.Precision.HIGHEST,
        preferred_element_type=jnp.float32,
    ).reshape(field.shape)
    return (
        field
        + mixing
        + eastward[None] * (widened[:, :, :-2] - widened[:, :, 2:]) * 0.5
        + northward[None] * (padded[:, :-2] - padded[:, 2:]) * 0.5
    )


def retreat(costate, vertical, eastward, northward):
    zonal = with_rim(eastward[None] * costate)
    lon_part = (zonal[:, :, 2:] - zonal[:, :, :-2]) * 0.5
    merid = jnp.pad(northward[None] * costate, ((0, 0), (1, 1), (0, 0)))
    lat_part = (merid[:, 2:] - merid[:, :-2]) * 0.5
    mixing = jnp.dot(
        vertical.T,
        costate.reshape(costate.shape[0], -1),
        precision=lax.Precision.HIGHEST,
        preferred_element_type=jnp.float32,
    ).reshape(costate.shape)
    return costate + mixing + lon_part + lat_part


def bias_of(rates, pushes, mine):
    order = lax.broadcasted_iota(jnp.int32, rates.shape, 0)
    masked = jnp.where(order <= mine, rates, 1.0)
    through = lax.cumprod(masked, axis=0, reverse=True)
    after = jnp.concatenate([through[1:], jnp.ones_like(through[:1])], axis=0)
    return jnp.sum(jnp.where(order <= mine, after * pushes, 0.0), axis=0)


def carried_back(rates, means, mine):
    order = lax.broadcasted_iota(jnp.int32, rates.shape, 0)
    masked = jnp.where(order > mine, rates, 1.0)
    through = lax.cumprod(masked, axis=0)
    return jnp.sum(jnp.where(order >= mine, through * means, 0.0), axis=0)


def shards_body(
    increment,
    vertical,
    east_wind,
    north_wind,
    error_weight,
    decay,
    forcing,
    obs_column,
    obs_count,
    obs_weight,
    obs_rinv,
    obs_depart,
):
    levels = increment.shape[1]
    lat_rows = increment.shape[2]
    lon_cols = increment.shape[3]
    tm_count = lax.axis_size("tm")
    slot_total = obs_column.shape[1]
    slot_cap = slot_total // tm_count
    mine = lax.axis_index("tm")
    both = gathered(jnp.stack([decay[0], forcing[0]]), "tm")
    all_rates = both[:, 0]
    bias = bias_of(all_rates, both[:, 1], mine)
    start = increment[0] + bias[:, None, None]
    mixer = vertical[0]
    eastward = east_wind[0]
    northward = north_wind[0]
    at_owner = jnp.concatenate([obs_weight[0], obs_rinv[0][None], obs_depart[0][None]])
    at_source = lax.all_to_all(at_owner, "tm", split_axis=1, concat_axis=1, tiled=True)
    weights = at_source[:levels]
    rinv = at_source[levels]
    depart = at_source[levels + 1]
    final = start
    for _ in range(STEPS):
        final = advance(final, mixer, eastward, northward)
    earlier = passed_along(final, "tm", 1)
    weighted = error_weight[0][:, None, None] * (start - earlier)
    flattened = final.reshape(levels, lat_rows * lon_cols)
    columns = obs_column[0]
    live = (jnp.arange(slot_total) % slot_cap < jnp.repeat(obs_count[0], slot_cap)).astype(
        jnp.float32
    )
    profiles = jnp.take(flattened, columns, axis=1) * live[None, :]
    seen = jnp.sum(weights * profiles, axis=0)
    equiv = lax.all_to_all(seen, "tm", split_axis=0, concat_axis=0, tiled=True)
    returned = weights * (rinv * (seen - depart))[None, :]
    adjoint_prof = returned * live[None, :]
    adjoint_end = (
        jnp.zeros((levels, lat_rows * lon_cols), jnp.float32)
        .at[:, columns]
        .add(adjoint_prof)
        .reshape(levels, lat_rows, lon_cols)
    )
    following = passed_along(weighted, "tm", -1)
    costate = adjoint_end - following
    for _ in range(STEPS):
        costate = retreat(costate, mixer, eastward, northward)
    gradient = weighted + costate
    partial_mean = jnp.sum(gradient, axis=(1, 2)) / (lat_rows * lon_cols * lax.axis_size("tile"))
    pieces = gathered(partial_mean, ("tm", "tile")).reshape(tm_count, -1, levels)
    grad_forcing = carried_back(all_rates, jnp.sum(pieces, axis=1), mine)
    return (gradient[None], grad_forcing[None], equiv[None])


def solution(mesh):
    placed = (
        P("tm", None, None, "tile"),
        P("tm", None, None),
        P("tm", None, "tile"),
        P("tm", None, "tile"),
        P("tm", None),
        P("tm", None),
        P("tm", None),
        P("tm", "tile"),
        P("tm", "tile"),
        P("tm", None, "tile"),
        P("tm", "tile"),
        P("tm", "tile"),
    )
    return jax.shard_map(
        shards_body,
        mesh=mesh,
        in_specs=placed,
        out_specs=(P("tm", None, None, "tile"), P("tm", None), P("tm", "tile")),
        check_vma=False,
    )
```

```python
import jax
import jax.numpy as jnp
from jax import lax
from jax.sharding import PartitionSpec as P


STEPS = 2


def padded_2(block, sides, width):
    for axis, dim in sides:
        count = lax.axis_size(axis)
        forward = [(i, i + 1) for i in range(count - 1)]
        forward.append((count - 1, 0))
        backward = [(target, source) for source, target in forward]
        low = lax.ppermute(
            lax.slice_in_dim(block, block.shape[dim] - width, None, axis=dim), axis, forward
        )
        high = lax.ppermute(lax.slice_in_dim(block, 0, width, axis=dim), axis, backward)
        block = jnp.concatenate([low, block, high], axis=dim)
    return block


def gathered(value, axis):
    count = lax.axis_size(axis)
    spread = jnp.broadcast_to(value[None], (count,) + value.shape)
    return lax.all_to_all(spread, axis, 0, 0, tiled=True)


def passed_along(value, axis, by):
    peers = lax.axis_size(axis)
    pairs = [(i, i + by) for i in range(peers) if 0 <= i + by < peers]
    return lax.ppermute(value, axis, pairs)


def with_rim(field):
    return padded_2(field, (("tile", 2),), 1)


def advance(field, vertical, eastward, northward):
    widened = with_rim(field)
    padded = jnp.pad(field, ((0, 0), (1, 1), (0, 0)))
    mixing = jnp.dot(
        vertical,
        field.reshape(field.shape[0], -1),
        precision=lax.Precision.HIGH,
        preferred_element_type=jnp.float32,
    ).reshape(field.shape)
    return (
        field
        + mixing
        + eastward[None] * (widened[:, :, :-2] - widened[:, :, 2:]) * 0.5
        + northward[None] * (padded[:, :-2] - padded[:, 2:]) * 0.5
    )


def retreat(costate, vertical, eastward, northward):
    zonal = with_rim(eastward[None] * costate)
    lon_part = (zonal[:, :, 2:] - zonal[:, :, :-2]) * 0.5
    merid = jnp.pad(northward[None] * costate, ((0, 0), (1, 1), (0, 0)))
    lat_part = (merid[:, 2:] - merid[:, :-2]) * 0.5
    mixing = jnp.dot(
        vertical.T,
        costate.reshape(costate.shape[0], -1),
        precision=lax.Precision.HIGH,
        preferred_element_type=jnp.float32,
    ).reshape(costate.shape)
    return costate + mixing + lon_part + lat_part


def bias_of(rates, pushes, mine):
    order = lax.broadcasted_iota(jnp.int32, rates.shape, 0)
    masked = jnp.where(order <= mine, rates, 1.0)
    through = lax.cumprod(masked, axis=0, reverse=True)
    after = jnp.concatenate([through[1:], jnp.ones_like(through[:1])], axis=0)
    return jnp.sum(jnp.where(order <= mine, after * pushes, 0.0), axis=0)


def carried_back(rates, means, mine):
    order = lax.broadcasted_iota(jnp.int32, rates.shape, 0)
    masked = jnp.where(order > mine, rates, 1.0)
    through = lax.cumprod(masked, axis=0)
    return jnp.sum(jnp.where(order >= mine, through * means, 0.0), axis=0)


def shards_body(
    increment,
    vertical,
    east_wind,
    north_wind,
    error_weight,
    decay,
    forcing,
    obs_column,
    obs_count,
    obs_weight,
    obs_rinv,
    obs_depart,
):
    levels = increment.shape[1]
    lat_rows = increment.shape[2]
    lon_cols = increment.shape[3]
    tm_count = lax.axis_size("tm")
    slot_total = obs_column.shape[1]
    slot_cap = slot_total // tm_count
    mine = lax.axis_index("tm")
    both = gathered(jnp.stack([decay[0], forcing[0]]), "tm")
    all_rates = both[:, 0]
    bias = bias_of(all_rates, both[:, 1], mine)
    start = increment[0] + bias[:, None, None]
    mixer = vertical[0]
    eastward = east_wind[0]
    northward = north_wind[0]
    at_owner = jnp.concatenate([obs_weight[0], obs_rinv[0][None], obs_depart[0][None]])
    at_source = lax.all_to_all(at_owner, "tm", split_axis=1, concat_axis=1, tiled=True)
    weights = at_source[:levels]
    rinv = at_source[levels]
    depart = at_source[levels + 1]
    final = start
    for _ in range(STEPS):
        final = advance(final, mixer, eastward, northward)
    earlier = passed_along(final, "tm", 1)
    weighted = error_weight[0][:, None, None] * (start - earlier)
    flattened = final.reshape(levels, lat_rows * lon_cols)
    columns = obs_column[0]
    live = (jnp.arange(slot_total) % slot_cap < jnp.repeat(obs_count[0], slot_cap)).astype(
        jnp.float32
    )
    profiles = jnp.take(flattened, columns, axis=1) * live[None, :]
    seen = jnp.sum(weights * profiles, axis=0)
    returned = weights * (rinv * (seen - depart))[None, :]
    adjoint_prof = returned * live[None, :]
    adjoint_end = (
        jnp.zeros((levels, lat_rows * lon_cols), jnp.float32)
        .at[:, columns]
        .add(adjoint_prof)
        .reshape(levels, lat_rows, lon_cols)
    )
    following = passed_along(weighted, "tm", -1)
    costate = adjoint_end - following
    for _ in range(STEPS):
        costate = retreat(costate, mixer, eastward, northward)
    gradient = weighted + costate
    partial_mean = jnp.sum(gradient, axis=(1, 2)) / (lat_rows * lon_cols * lax.axis_size("tile"))
    tile_count = lax.axis_size("tile")
    owed = jnp.repeat(seen.reshape(tm_count, 1, slot_cap), tile_count, axis=1)
    leaving = jnp.concatenate(
        [jnp.broadcast_to(partial_mean, (tm_count, tile_count, levels)), owed], axis=2
    )
    pieces = lax.all_to_all(
        leaving.reshape(tm_count * tile_count, -1), ("tm", "tile"), 0, 0, tiled=True
    ).reshape(tm_count, tile_count, -1)
    grad_forcing = carried_back(all_rates, jnp.sum(pieces[:, :, :levels], axis=1), mine)
    own_tile = lax.dynamic_index_in_dim(pieces, lax.axis_index("tile"), axis=1, keepdims=False)
    equiv = own_tile[:, levels:].reshape(-1)
    return (gradient[None], grad_forcing[None], equiv[None])


def solution(mesh):
    placed = (
        P("tm", None, None, "tile"),
        P("tm", None, None),
        P("tm", None, "tile"),
        P("tm", None, "tile"),
        P("tm", None),
        P("tm", None),
        P("tm", None),
        P("tm", "tile"),
        P("tm", "tile"),
        P("tm", None, "tile"),
        P("tm", "tile"),
        P("tm", "tile"),
    )
    return jax.shard_map(
        shards_body,
        mesh=mesh,
        in_specs=placed,
        out_specs=(P("tm", None, None, "tile"), P("tm", None), P("tm", "tile")),
        check_vma=False,
    )
```

```python
import jax
import jax.numpy as jnp
from jax import lax
from jax.sharding import PartitionSpec as P


STEPS = 2


def gathered(value, axis):
    count = lax.axis_size(axis)
    spread = jnp.broadcast_to(value[None], (count,) + value.shape)
    return lax.all_to_all(spread, axis, 0, 0, tiled=True)


def passed_along(value, axis, by):
    peers = lax.axis_size(axis)
    pairs = [(i, i + by) for i in range(peers) if 0 <= i + by < peers]
    return lax.ppermute(value, axis, pairs)


def with_rim(field):
    count = lax.axis_size("tile")
    forward = [(i, (i + 1) % count) for i in range(count)]
    backward = [(target, source) for source, target in forward]
    width = field.shape[2]
    low = lax.ppermute(field[:, :, width - 1 :], "tile", forward)
    high = lax.ppermute(field[:, :, :1], "tile", backward)
    lon = lax.broadcasted_iota(jnp.int32, field.shape, 2)
    west = jnp.where(lon == 0, low, jnp.roll(field, 1, axis=2))
    east = jnp.where(lon == width - 1, high, jnp.roll(field, -1, axis=2))
    return west, east


def advance(field, vertical, eastward, northward):
    west, east = with_rim(field)
    padded = jnp.pad(field, ((0, 0), (1, 1), (0, 0)))
    mixing = jnp.dot(
        vertical,
        field.reshape(field.shape[0], -1),
        precision=lax.Precision.HIGH,
        preferred_element_type=jnp.float32,
    ).reshape(field.shape)
    return (
        field
        + mixing
        + eastward[None] * (west - east) * 0.5
        + northward[None] * (padded[:, :-2] - padded[:, 2:]) * 0.5
    )


def retreat(costate, vertical, eastward, northward):
    west, east = with_rim(eastward[None] * costate)
    lon_part = (east - west) * 0.5
    merid = jnp.pad(northward[None] * costate, ((0, 0), (1, 1), (0, 0)))
    lat_part = (merid[:, 2:] - merid[:, :-2]) * 0.5
    mixing = jnp.dot(
        vertical.T,
        costate.reshape(costate.shape[0], -1),
        precision=lax.Precision.HIGH,
        preferred_element_type=jnp.float32,
    ).reshape(costate.shape)
    return costate + mixing + lon_part + lat_part


def bias_of(rates, pushes, mine):
    order = lax.broadcasted_iota(jnp.int32, rates.shape, 0)
    masked = jnp.where(order <= mine, rates, 1.0)
    through = lax.cumprod(masked, axis=0, reverse=True)
    after = jnp.concatenate([through[1:], jnp.ones_like(through[:1])], axis=0)
    return jnp.sum(jnp.where(order <= mine, after * pushes, 0.0), axis=0)


def carried_back(rates, means, mine):
    order = lax.broadcasted_iota(jnp.int32, rates.shape, 0)
    masked = jnp.where(order > mine, rates, 1.0)
    through = lax.cumprod(masked, axis=0)
    return jnp.sum(jnp.where(order >= mine, through * means, 0.0), axis=0)


def shards_body(
    increment,
    vertical,
    east_wind,
    north_wind,
    error_weight,
    decay,
    forcing,
    obs_column,
    obs_count,
    obs_weight,
    obs_rinv,
    obs_depart,
):
    levels = increment.shape[1]
    lat_rows = increment.shape[2]
    lon_cols = increment.shape[3]
    tm_count = lax.axis_size("tm")
    slot_total = obs_column.shape[1]
    slot_cap = slot_total // tm_count
    mine = lax.axis_index("tm")
    both = gathered(jnp.stack([decay[0], forcing[0]]), "tm")
    all_rates = both[:, 0]
    bias = bias_of(all_rates, both[:, 1], mine)
    start = increment[0] + bias[:, None, None]
    mixer = vertical[0]
    eastward = east_wind[0]
    northward = north_wind[0]
    at_owner = jnp.concatenate([obs_weight[0], obs_rinv[0][None], obs_depart[0][None]])
    at_source = lax.all_to_all(at_owner, "tm", split_axis=1, concat_axis=1, tiled=True)
    weights = at_source[:levels]
    rinv = at_source[levels]
    depart = at_source[levels + 1]
    final = start
    for _ in range(STEPS):
        final = advance(final, mixer, eastward, northward)
    earlier = passed_along(final, "tm", 1)
    weighted = error_weight[0][:, None, None] * (start - earlier)
    flattened = final.reshape(levels, lat_rows * lon_cols)
    columns = obs_column[0]
    live = (jnp.arange(slot_total) % slot_cap < jnp.repeat(obs_count[0], slot_cap)).astype(
        jnp.float32
    )
    profiles = jnp.take(flattened, columns, axis=1) * live[None, :]
    seen = jnp.sum(weights * profiles, axis=0)
    returned = weights * (rinv * (seen - depart))[None, :]
    adjoint_prof = returned * live[None, :]
    adjoint_end = (
        jnp.zeros((levels, lat_rows * lon_cols), jnp.float32)
        .at[:, columns]
        .add(adjoint_prof)
        .reshape(levels, lat_rows, lon_cols)
    )
    following = passed_along(weighted, "tm", -1)
    costate = adjoint_end - following
    for _ in range(STEPS):
        costate = retreat(costate, mixer, eastward, northward)
    gradient = weighted + costate
    partial_mean = jnp.sum(gradient, axis=(1, 2)) / (lat_rows * lon_cols * lax.axis_size("tile"))
    tile_count = lax.axis_size("tile")
    owed = jnp.repeat(seen.reshape(tm_count, 1, slot_cap), tile_count, axis=1)
    leaving = jnp.concatenate(
        [jnp.broadcast_to(partial_mean, (tm_count, tile_count, levels)), owed], axis=2
    )
    pieces = lax.all_to_all(
        leaving.reshape(tm_count * tile_count, -1), ("tm", "tile"), 0, 0, tiled=True
    ).reshape(tm_count, tile_count, -1)
    grad_forcing = carried_back(all_rates, jnp.sum(pieces[:, :, :levels], axis=1), mine)
    own_tile = lax.dynamic_index_in_dim(pieces, lax.axis_index("tile"), axis=1, keepdims=False)
    equiv = own_tile[:, levels:].reshape(-1)
    return (gradient[None], grad_forcing[None], equiv[None])


def solution(mesh):
    placed = (
        P("tm", None, None, "tile"),
        P("tm", None, None),
        P("tm", None, "tile"),
        P("tm", None, "tile"),
        P("tm", None),
        P("tm", None),
        P("tm", None),
        P("tm", "tile"),
        P("tm", "tile"),
        P("tm", None, "tile"),
        P("tm", "tile"),
        P("tm", "tile"),
    )
    return jax.shard_map(
        shards_body,
        mesh=mesh,
        in_specs=placed,
        out_specs=(P("tm", None, None, "tile"), P("tm", None), P("tm", "tile")),
        check_vma=False,
    )
```

```python
import jax
import jax.numpy as jnp
from jax import lax
from jax.sharding import PartitionSpec as P


STEPS = 2


def padded_2(block, sides, width):
    for axis, dim in sides:
        count = lax.axis_size(axis)
        forward = [(i, i + 1) for i in range(count - 1)]
        forward.append((count - 1, 0))
        backward = [(target, source) for source, target in forward]
        low = lax.ppermute(
            lax.slice_in_dim(block, block.shape[dim] - width, None, axis=dim), axis, forward
        )
        high = lax.ppermute(lax.slice_in_dim(block, 0, width, axis=dim), axis, backward)
        block = jnp.concatenate([low, block, high], axis=dim)
    return block


def gathered(value, axis):
    count = lax.axis_size(axis)
    spread = jnp.broadcast_to(value[None], (count,) + value.shape)
    return lax.all_to_all(spread, axis, 0, 0, tiled=True)


def passed_along(value, axis, by):
    peers = lax.axis_size(axis)
    pairs = [(i, i + by) for i in range(peers) if 0 <= i + by < peers]
    return lax.ppermute(value, axis, pairs)


def with_rim(field):
    return padded_2(field, (("tile", 2),), 1)


def advance(field, vertical, eastward, northward):
    widened = with_rim(field)
    padded = jnp.pad(field, ((0, 0), (1, 1), (0, 0)))
    mixing = jnp.dot(
        vertical,
        field.reshape(field.shape[0], -1),
        precision=lax.Precision.HIGH,
        preferred_element_type=jnp.float32,
    ).reshape(field.shape)
    return (
        field
        + mixing
        + eastward[None] * (widened[:, :, :-2] - widened[:, :, 2:]) * 0.5
        + northward[None] * (padded[:, :-2] - padded[:, 2:]) * 0.5
    )


def retreat(costate, vertical, eastward, northward):
    zonal = with_rim(eastward[None] * costate)
    lon_part = (zonal[:, :, 2:] - zonal[:, :, :-2]) * 0.5
    merid = jnp.pad(northward[None] * costate, ((0, 0), (1, 1), (0, 0)))
    lat_part = (merid[:, 2:] - merid[:, :-2]) * 0.5
    mixing = jnp.dot(
        vertical.T,
        costate.reshape(costate.shape[0], -1),
        precision=lax.Precision.HIGH,
        preferred_element_type=jnp.float32,
    ).reshape(costate.shape)
    return costate + mixing + lon_part + lat_part


def bias_of(rates, pushes, mine):
    order = lax.broadcasted_iota(jnp.int32, rates.shape, 0)
    masked = jnp.where(order <= mine, rates, 1.0)
    through = lax.cumprod(masked, axis=0, reverse=True)
    after = jnp.concatenate([through[1:], jnp.ones_like(through[:1])], axis=0)
    return jnp.sum(jnp.where(order <= mine, after * pushes, 0.0), axis=0)


def carried_back(rates, means, mine):
    order = lax.broadcasted_iota(jnp.int32, rates.shape, 0)
    masked = jnp.where(order > mine, rates, 1.0)
    through = lax.cumprod(masked, axis=0)
    return jnp.sum(jnp.where(order >= mine, through * means, 0.0), axis=0)


def shards_body(
    increment,
    vertical,
    east_wind,
    north_wind,
    error_weight,
    decay,
    forcing,
    obs_column,
    obs_count,
    obs_weight,
    obs_rinv,
    obs_depart,
):
    levels = increment.shape[1]
    lat_rows = increment.shape[2]
    lon_cols = increment.shape[3]
    tm_count = lax.axis_size("tm")
    slot_total = obs_column.shape[1]
    slot_cap = slot_total // tm_count
    mine = lax.axis_index("tm")
    both = gathered(jnp.stack([decay[0], forcing[0]]), "tm")
    all_rates = both[:, 0]
    bias = bias_of(all_rates, both[:, 1], mine)
    start = increment[0] + bias[:, None, None]
    mixer = vertical[0]
    eastward = east_wind[0]
    northward = north_wind[0]
    at_owner = jnp.concatenate([obs_weight[0], obs_rinv[0][None], obs_depart[0][None]])
    at_source = lax.all_to_all(at_owner, "tm", split_axis=1, concat_axis=1, tiled=True)
    weights = at_source[:levels]
    rinv = at_source[levels]
    depart = at_source[levels + 1]
    final = start
    for _ in range(STEPS):
        final = advance(final, mixer, eastward, northward)
    earlier = passed_along(final, "tm", 1)
    weighted = error_weight[0][:, None, None] * (start - earlier)
    flattened = final.reshape(levels, lat_rows * lon_cols)
    columns = obs_column[0]
    live = (jnp.arange(slot_total) % slot_cap < jnp.repeat(obs_count[0], slot_cap)).astype(
        jnp.float32
    )
    picks = (
        lax.broadcasted_iota(jnp.int32, (slot_total, lat_rows * lon_cols), 1) == columns[:, None]
    ).astype(jnp.float32)
    profiles = jnp.dot(
        flattened, picks.T, precision=lax.Precision.HIGH, preferred_element_type=jnp.float32
    ) * live[None, :]
    seen = jnp.sum(weights * profiles, axis=0)
    returned = weights * (rinv * (seen - depart))[None, :]
    adjoint_prof = returned * live[None, :]
    adjoint_end = jnp.dot(
        adjoint_prof, picks, precision=lax.Precision.HIGH, preferred_element_type=jnp.float32
    ).reshape(levels, lat_rows, lon_cols)
    following = passed_along(weighted, "tm", -1)
    costate = adjoint_end - following
    for _ in range(STEPS):
        costate = retreat(costate, mixer, eastward, northward)
    gradient = weighted + costate
    partial_mean = jnp.sum(gradient, axis=(1, 2)) / (lat_rows * lon_cols * lax.axis_size("tile"))
    tile_count = lax.axis_size("tile")
    owed = jnp.repeat(seen.reshape(tm_count, 1, slot_cap), tile_count, axis=1)
    leaving = jnp.concatenate(
        [jnp.broadcast_to(partial_mean, (tm_count, tile_count, levels)), owed], axis=2
    )
    pieces = lax.all_to_all(
        leaving.reshape(tm_count * tile_count, -1), ("tm", "tile"), 0, 0, tiled=True
    ).reshape(tm_count, tile_count, -1)
    grad_forcing = carried_back(all_rates, jnp.sum(pieces[:, :, :levels], axis=1), mine)
    own_tile = lax.dynamic_index_in_dim(pieces, lax.axis_index("tile"), axis=1, keepdims=False)
    equiv = own_tile[:, levels:].reshape(-1)
    return (gradient[None], grad_forcing[None], equiv[None])


def solution(mesh):
    placed = (
        P("tm", None, None, "tile"),
        P("tm", None, None),
        P("tm", None, "tile"),
        P("tm", None, "tile"),
        P("tm", None),
        P("tm", None),
        P("tm", None),
        P("tm", "tile"),
        P("tm", "tile"),
        P("tm", None, "tile"),
        P("tm", "tile"),
        P("tm", "tile"),
    )
    return jax.shard_map(
        shards_body,
        mesh=mesh,
        in_specs=placed,
        out_specs=(P("tm", None, None, "tile"), P("tm", None), P("tm", "tile")),
        check_vma=False,
    )
```

```python
import jax
import jax.numpy as jnp
from jax import lax
from jax.sharding import PartitionSpec as P


STEPS = 2


def padded_2(block, sides, width):
    for axis, dim in sides:
        count = lax.axis_size(axis)
        forward = [(i, i + 1) for i in range(count - 1)]
        forward.append((count - 1, 0))
        backward = [(target, source) for source, target in forward]
        low = lax.ppermute(
            lax.slice_in_dim(block, block.shape[dim] - width, None, axis=dim), axis, forward
        )
        high = lax.ppermute(lax.slice_in_dim(block, 0, width, axis=dim), axis, backward)
        block = jnp.concatenate([low, block, high], axis=dim)
    return block


def gathered(value, axis):
    count = lax.axis_size(axis)
    spread = jnp.broadcast_to(value[None], (count,) + value.shape)
    return lax.all_to_all(spread, axis, 0, 0, tiled=True)


def passed_along(value, axis, by):
    peers = lax.axis_size(axis)
    pairs = [(i, i + by) for i in range(peers) if 0 <= i + by < peers]
    return lax.ppermute(value, axis, pairs)


def with_rim(field):
    return padded_2(field, (("tile", 2),), 1)


def advance(field, vertical, eastward, northward):
    widened = with_rim(field)
    padded = jnp.pad(field, ((0, 0), (1, 1), (0, 0)))
    mixing = jnp.dot(
        vertical,
        field.reshape(field.shape[0], -1),
        precision=lax.Precision.HIGH,
        preferred_element_type=jnp.float32,
    ).reshape(field.shape)
    return (
        field
        + mixing
        + eastward[None] * (widened[:, :, :-2] - widened[:, :, 2:]) * 0.5
        + northward[None] * (padded[:, :-2] - padded[:, 2:]) * 0.5
    )


def retreat(costate, vertical, eastward, northward):
    zonal = with_rim(eastward[None] * costate)
    lon_part = (zonal[:, :, 2:] - zonal[:, :, :-2]) * 0.5
    merid = jnp.pad(northward[None] * costate, ((0, 0), (1, 1), (0, 0)))
    lat_part = (merid[:, 2:] - merid[:, :-2]) * 0.5
    mixing = jnp.dot(
        vertical.T,
        costate.reshape(costate.shape[0], -1),
        precision=lax.Precision.HIGH,
        preferred_element_type=jnp.float32,
    ).reshape(costate.shape)
    return costate + mixing + lon_part + lat_part


def bias_of(rates, pushes, mine):
    order = lax.broadcasted_iota(jnp.int32, rates.shape, 0)
    masked = jnp.where(order <= mine, rates, 1.0)
    through = lax.cumprod(masked, axis=0, reverse=True)
    after = jnp.concatenate([through[1:], jnp.ones_like(through[:1])], axis=0)
    return jnp.sum(jnp.where(order <= mine, after * pushes, 0.0), axis=0)


def carried_back(rates, means, mine):
    order = lax.broadcasted_iota(jnp.int32, rates.shape, 0)
    masked = jnp.where(order > mine, rates, 1.0)
    through = lax.cumprod(masked, axis=0)
    return jnp.sum(jnp.where(order >= mine, through * means, 0.0), axis=0)


def shards_body(
    increment,
    vertical,
    east_wind,
    north_wind,
    error_weight,
    decay,
    forcing,
    obs_column,
    obs_count,
    obs_weight,
    obs_rinv,
    obs_depart,
):
    levels = increment.shape[1]
    lat_rows = increment.shape[2]
    lon_cols = increment.shape[3]
    tm_count = lax.axis_size("tm")
    slot_total = obs_column.shape[1]
    slot_cap = slot_total // tm_count
    mine = lax.axis_index("tm")
    both = gathered(jnp.stack([decay[0], forcing[0]]), "tm")
    all_rates = both[:, 0]
    bias = bias_of(all_rates, both[:, 1], mine)
    start = increment[0] + bias[:, None, None]
    mixer = vertical[0]
    eastward = east_wind[0]
    northward = north_wind[0]
    at_owner = jnp.concatenate([obs_weight[0], obs_rinv[0][None], obs_depart[0][None]])
    at_source = lax.all_to_all(at_owner, "tm", split_axis=1, concat_axis=1, tiled=True)
    weights = at_source[:levels]
    rinv = at_source[levels]
    depart = at_source[levels + 1]
    final = start
    for _ in range(STEPS):
        final = advance(final, mixer, eastward, northward)
    later_start = passed_along(start, "tm", -1)
    earlier = passed_along(final, "tm", 1)
    weighted = error_weight[0][:, None, None] * (start - earlier)
    flattened = final.reshape(levels, lat_rows * lon_cols)
    columns = obs_column[0]
    live = (jnp.arange(slot_total) % slot_cap < jnp.repeat(obs_count[0], slot_cap)).astype(
        jnp.float32
    )
    picks = (
        lax.broadcasted_iota(jnp.int32, (slot_total, lat_rows * lon_cols), 1) == columns[:, None]
    ).astype(jnp.float32)
    profiles = jnp.dot(
        flattened, picks.T, precision=lax.Precision.HIGHEST, preferred_element_type=jnp.float32
    ) * live[None, :]
    seen = jnp.sum(weights * profiles, axis=0)
    returned = weights * (rinv * (seen - depart))[None, :]
    adjoint_prof = returned * live[None, :]
    adjoint_end = jnp.dot(
        adjoint_prof, picks, precision=lax.Precision.HIGHEST, preferred_element_type=jnp.float32
    ).reshape(levels, lat_rows, lon_cols)
    later_weight = passed_along(error_weight[0], "tm", -1)
    following = later_weight[:, None, None] * (later_start - final)
    costate = adjoint_end - following
    for _ in range(STEPS):
        costate = retreat(costate, mixer, eastward, northward)
    gradient = weighted + costate
    partial_mean = jnp.sum(gradient, axis=(1, 2)) / (lat_rows * lon_cols * lax.axis_size("tile"))
    tile_count = lax.axis_size("tile")
    owed = jnp.repeat(seen.reshape(tm_count, 1, slot_cap), tile_count, axis=1)
    leaving = jnp.concatenate(
        [jnp.broadcast_to(partial_mean, (tm_count, tile_count, levels)), owed], axis=2
    )
    pieces = lax.all_to_all(
        leaving.reshape(tm_count * tile_count, -1), ("tm", "tile"), 0, 0, tiled=True
    ).reshape(tm_count, tile_count, -1)
    grad_forcing = carried_back(all_rates, jnp.sum(pieces[:, :, :levels], axis=1), mine)
    own_tile = lax.dynamic_index_in_dim(pieces, lax.axis_index("tile"), axis=1, keepdims=False)
    equiv = own_tile[:, levels:].reshape(-1)
    return (gradient[None], grad_forcing[None], equiv[None])


def solution(mesh):
    placed = (
        P("tm", None, None, "tile"),
        P("tm", None, None),
        P("tm", None, "tile"),
        P("tm", None, "tile"),
        P("tm", None),
        P("tm", None),
        P("tm", None),
        P("tm", "tile"),
        P("tm", "tile"),
        P("tm", None, "tile"),
        P("tm", "tile"),
        P("tm", "tile"),
    )
    return jax.shard_map(
        shards_body,
        mesh=mesh,
        in_specs=placed,
        out_specs=(P("tm", None, None, "tile"), P("tm", None), P("tm", "tile")),
        check_vma=False,
    )
```

```python
import jax
import jax.numpy as jnp
from jax import lax
from jax.sharding import PartitionSpec as P


STEPS = 2


def padded_2(block, sides, width):
    for axis, dim in sides:
        count = lax.axis_size(axis)
        forward = [(i, i + 1) for i in range(count - 1)]
        forward.append((count - 1, 0))
        backward = [(target, source) for source, target in forward]
        low = lax.ppermute(
            lax.slice_in_dim(block, block.shape[dim] - width, None, axis=dim), axis, forward
        )
        high = lax.ppermute(lax.slice_in_dim(block, 0, width, axis=dim), axis, backward)
        block = jnp.concatenate([low, block, high], axis=dim)
    return block


def gathered(value, axis):
    count = lax.axis_size(axis)
    spread = jnp.broadcast_to(value[None], (count,) + value.shape)
    return lax.all_to_all(spread, axis, 0, 0, tiled=True)


def passed_along(value, axis, by):
    peers = lax.axis_size(axis)
    pairs = [(i, i + by) for i in range(peers) if 0 <= i + by < peers]
    return lax.ppermute(value, axis, pairs)


def with_rim(field):
    return padded_2(field, (("tile", 2),), 1)


def advance(field, vertical, eastward, northward):
    widened = with_rim(field)
    padded = jnp.pad(field, ((0, 0), (1, 1), (0, 0)))
    mixing = jnp.dot(
        vertical,
        field.reshape(field.shape[0], -1),
        precision=lax.Precision.HIGH,
        preferred_element_type=jnp.float32,
    ).reshape(field.shape)
    return (
        field
        + mixing
        + eastward[None] * (widened[:, :, :-2] - widened[:, :, 2:]) * 0.5
        + northward[None] * (padded[:, :-2] - padded[:, 2:]) * 0.5
    )


def retreat(costate, vertical, eastward, northward):
    zonal = with_rim(eastward[None] * costate)
    lon_part = (zonal[:, :, 2:] - zonal[:, :, :-2]) * 0.5
    merid = jnp.pad(northward[None] * costate, ((0, 0), (1, 1), (0, 0)))
    lat_part = (merid[:, 2:] - merid[:, :-2]) * 0.5
    mixing = jnp.dot(
        vertical.T,
        costate.reshape(costate.shape[0], -1),
        precision=lax.Precision.HIGH,
        preferred_element_type=jnp.float32,
    ).reshape(costate.shape)
    return costate + mixing + lon_part + lat_part


def bias_of(rates, pushes, mine):
    order = lax.broadcasted_iota(jnp.int32, rates.shape, 0)
    masked = jnp.where(order <= mine, rates, 1.0)
    through = lax.cumprod(masked, axis=0, reverse=True)
    after = jnp.concatenate([through[1:], jnp.ones_like(through[:1])], axis=0)
    return jnp.sum(jnp.where(order <= mine, after * pushes, 0.0), axis=0)


def carried_back(rates, means, mine):
    order = lax.broadcasted_iota(jnp.int32, rates.shape, 0)
    masked = jnp.where(order > mine, rates, 1.0)
    through = lax.cumprod(masked, axis=0)
    return jnp.sum(jnp.where(order >= mine, through * means, 0.0), axis=0)


def shards_body(
    increment,
    vertical,
    east_wind,
    north_wind,
    error_weight,
    decay,
    forcing,
    obs_column,
    obs_count,
    obs_weight,
    obs_rinv,
    obs_depart,
):
    levels = increment.shape[1]
    lat_rows = increment.shape[2]
    lon_cols = increment.shape[3]
    tm_count = lax.axis_size("tm")
    slot_total = obs_column.shape[1]
    slot_cap = slot_total // tm_count
    mine = lax.axis_index("tm")
    both = gathered(jnp.stack([decay[0], forcing[0]]), "tm")
    all_rates = both[:, 0]
    bias = bias_of(all_rates, both[:, 1], mine)
    start = increment[0] + bias[:, None, None]
    mixer = vertical[0]
    eastward = east_wind[0]
    northward = north_wind[0]
    at_owner = jnp.concatenate([obs_weight[0], obs_rinv[0][None], obs_depart[0][None]])
    at_source = lax.all_to_all(at_owner, "tm", split_axis=1, concat_axis=1, tiled=True)
    weights = at_source[:levels]
    rinv = at_source[levels]
    depart = at_source[levels + 1]
    final = start
    for _ in range(STEPS):
        final = advance(final, mixer, eastward, northward)
    later_start = passed_along(start, "tm", -1)
    earlier = passed_along(final, "tm", 1)
    weighted = error_weight[0][:, None, None] * (start - earlier)
    flattened = final.reshape(levels, lat_rows * lon_cols)
    columns = obs_column[0]
    live = (jnp.arange(slot_total) % slot_cap < jnp.repeat(obs_count[0], slot_cap)).astype(
        jnp.float32
    )
    picks = (
        lax.broadcasted_iota(jnp.int32, (slot_total, lat_rows * lon_cols), 1) == columns[:, None]
    ).astype(jnp.float32) * live[:, None]
    profiles = jnp.dot(
        flattened, picks.T, precision=lax.Precision.HIGHEST, preferred_element_type=jnp.float32
    )
    seen = jnp.sum(weights * profiles, axis=0)
    returned = weights * (rinv * (seen - depart))[None, :]
    adjoint_end = jnp.dot(
        returned, picks, precision=lax.Precision.HIGHEST, preferred_element_type=jnp.float32
    ).reshape(levels, lat_rows, lon_cols)
    later_weight = passed_along(error_weight[0], "tm", -1)
    following = later_weight[:, None, None] * (later_start - final)
    costate = adjoint_end - following
    for _ in range(STEPS):
        costate = retreat(costate, mixer, eastward, northward)
    gradient = weighted + costate
    partial_mean = jnp.sum(gradient, axis=(1, 2)) / (lat_rows * lon_cols * lax.axis_size("tile"))
    tile_count = lax.axis_size("tile")
    owed = jnp.repeat(seen.reshape(tm_count, 1, slot_cap), tile_count, axis=1)
    leaving = jnp.concatenate(
        [jnp.broadcast_to(partial_mean, (tm_count, tile_count, levels)), owed], axis=2
    )
    pieces = lax.all_to_all(
        leaving.reshape(tm_count * tile_count, -1), ("tm", "tile"), 0, 0, tiled=True
    ).reshape(tm_count, tile_count, -1)
    grad_forcing = carried_back(all_rates, jnp.sum(pieces[:, :, :levels], axis=1), mine)
    own_tile = lax.dynamic_index_in_dim(pieces, lax.axis_index("tile"), axis=1, keepdims=False)
    equiv = own_tile[:, levels:].reshape(-1)
    return (gradient[None], grad_forcing[None], equiv[None])


def solution(mesh):
    placed = (
        P("tm", None, None, "tile"),
        P("tm", None, None),
        P("tm", None, "tile"),
        P("tm", None, "tile"),
        P("tm", None),
        P("tm", None),
        P("tm", None),
        P("tm", "tile"),
        P("tm", "tile"),
        P("tm", None, "tile"),
        P("tm", "tile"),
        P("tm", "tile"),
    )
    return jax.shard_map(
        shards_body,
        mesh=mesh,
        in_specs=placed,
        out_specs=(P("tm", None, None, "tile"), P("tm", None), P("tm", "tile")),
        check_vma=False,
    )
```
